32 devices in a mesh: ctx: 16 (over z, y, x), fsdp: 2 (over core).
Axes of the slice: x: 2, y: 2, z: 4, core: 2. Of those that a mesh axis runs over, the one named last changes fastest.
Arguments:
- xbc: bfloat16 [4096, 9216], P(('fsdp', 'ctx')), may hold values from -6 to 6
- dt: bfloat16 [4096, 128], P(('fsdp', 'ctx')), may hold values from -5 to 5
- conv_weight: float32 [4, 9216], P(None, 'fsdp'), may hold values from -3 to 3
- conv_bias: float32 [9216], P('fsdp'), may hold values from -0.5 to 0.5
- dt_bias: float32 [128], P('fsdp'), may hold values from -1 to 1
- a_log: float32 [128], P('fsdp'), may hold values from -14 to -3
- skip: float32 [128], P('fsdp'), may hold values from 0.5 to 2
- norm_gain: float32 [8192], P('fsdp'), may hold values from 0.5 to 1.5
Outputs:
- mixed: bfloat16 [4096, 8192], P(('fsdp', 'ctx'))
The draws below stay inside these ranges and needn't reach their ends.
All inputs are finite; a program needn't handle non-finite values.
Results may differ from the reference program's by a relative error of at most 0.0051.
Values may be sent and summed in bfloat16 or wider, within the bound.
A program may use at most 128 MiB of HBM per device.

```python
import jax
import jax.numpy as jnp
from jax import lax

HEADS = 128
P_SIZE = 64
N = 128
GROUPS = 4
DI = 8192
CH = 9216
LENGTH = 4096


def draw_a_log(key, part):
    pick_key, slow_key, fast_key = jax.random.split(jax.random.fold_in(key, 11), 3)
    share = 0.5
    fast_heads = jax.random.bernoulli(pick_key, share, (HEADS,))
    slow_rate = jnp.log(0.1 / LENGTH) + jax.random.uniform(slow_key, (HEADS,), jnp.float32) * jnp.log(15.0)
    fast_rate = jnp.log(0.015) + jax.random.uniform(fast_key, (HEADS,), jnp.float32) * jnp.log(3.0)
    return jnp.where(fast_heads, fast_rate, slow_rate).astype(jnp.float32)


def shard_levels(rng, extent, cuts, low, largest):
    level = 1.0
    for dim, shards_of in cuts:
        steps = jax.random.uniform(jax.random.fold_in(jax.random.fold_in(rng, 6), dim), (shards_of,), jnp.float32, low / len(cuts), largest / len(cuts))
        level = level * jnp.repeat(jnp.exp(steps), extent[dim] // shards_of).reshape((-1,) + (1,) * (len(extent) - 1 - dim))
    return level


def normal_values(key, shape, scale, reach, cuts=(), kind=jnp.bfloat16):
    values = jax.random.normal(key, shape, jnp.float32) * scale
    if len(cuts) > 0:
        values = shard_levels(key, shape, cuts, -0.22, 0.18) * values
    return jnp.clip(values, min=-reach, max=reach).astype(kind)


def setup_inputs(seed: int = 0) -> dict:
    key_of = jax.random.split(jax.random.key(seed), 9)
    return {
        "xbc": normal_values(key_of[0], (LENGTH, CH), 1.0, 6.0, ((0, 32),)),
        "dt": normal_values(key_of[1], (LENGTH, HEADS), 1.0, 5.0, ((0, 32),)),
        "conv_weight": normal_values(key_of[2], (4, CH), 4 ** -0.5, 3.0, ((1, 2),), jnp.float32),
        "conv_bias": jnp.clip(jax.random.uniform(key_of[3], (CH,), jnp.float32, -0.5, 0.5) * shard_levels(key_of[3], (CH,), ((0, 2),), -0.4, 0.0), -0.5, 0.5),
        "dt_bias": jnp.clip(jax.random.uniform(key_of[4], (HEADS,), jnp.float32, -1.0, 1.0) * shard_levels(key_of[4], (HEADS,), ((0, 2),), -0.4, 0.0), -1.0, 1.0),
        "a_log": draw_a_log(jax.random.fold_in(key_of[8], 71), 0),
        "skip": jnp.clip(0.5 + 1.5 * jax.random.uniform(key_of[6], (HEADS,), jnp.float32) ** shard_levels(key_of[6], (HEADS,), ((0, 2),), -0.2, 0.2), 0.5, 2.0),
        "norm_gain": jnp.clip(1.0 + 0.1 * jax.random.normal(key_of[7], (DI,), jnp.float32), 0.5, 1.5),
    }


PRECISE = lax.Precision.HIGHEST

def conv_silu(extended, taps, offsets):
    row_count = extended.shape[0] - 3
    total = offsets[None, :] + taps[0][None, :] * extended[0:row_count].astype(jnp.float32)
    for kernel_tap in range(1, 4):
        total = total + taps[kernel_tap][None, :] * extended[kernel_tap:kernel_tap + row_count].astype(jnp.float32)
    return jax.nn.silu(total).astype(jnp.bfloat16)

def span_terms(values, keys_in, queries, delta, decay, state):
    values_f = values.astype(jnp.float32)
    keys_f = keys_in.astype(jnp.float32)
    queries_f = queries.astype(jnp.float32)
    block_rows = values.shape[0]
    cumulative = jnp.cumsum(decay, axis=0)
    lower = (lax.broadcasted_iota(jnp.int32, (block_rows, block_rows), 0) >= lax.broadcasted_iota(jnp.int32, (block_rows, block_rows), 1))[:, :, None, None]
    spread = cumulative[:, None] - cumulative[None, :]
    segment = jnp.where(lower, jnp.exp(jnp.where(lower, spread, 0.0)), 0.0)
    scores = jnp.einsum('tgn,sgn->tsg', queries_f, keys_f, precision=PRECISE)
    weights = segment * scores[..., None] * delta[None]
    inner = jnp.einsum('tsgk,sgkp->tgkp', weights, values_f, precision=PRECISE)
    carried = jnp.exp(cumulative)[..., None] * jnp.einsum('tgn,gkpn->tgkp', queries_f, state, precision=PRECISE)
    tail_weight = jnp.exp(cumulative[-1][None] - cumulative) * delta
    updated = jnp.exp(cumulative[-1])[..., None, None] * state + jnp.einsum('sgk,sgn,sgkp->gkpn', tail_weight, keys_f, values_f, precision=PRECISE)
    return (inner + carried, updated)

def span_sweep(values, keys_in, queries, delta, decay, state, block_rows):
    blocks = values.shape[0] // block_rows

    def split_rows(array):
        return array.reshape((blocks, block_rows) + array.shape[1:])

    def advance(carry, pieces):
        result, updated = span_terms(pieces[0], pieces[1], pieces[2], pieces[3], pieces[4], carry)
        return (updated, result)
    last_state, results = lax.scan(advance, state, (split_rows(values), split_rows(keys_in), split_rows(queries), split_rows(delta), split_rows(decay)))
    return (results.reshape(values.shape), last_state)

def group_norm(mixed_in, gain):
    row_count = mixed_in.shape[0]
    values = mixed_in.astype(jnp.float32).reshape(row_count, GROUPS, -1)
    meansq = lax.optimization_barrier(jnp.mean(values * values, axis=-1, keepdims=True))
    scaled = values * lax.rsqrt(meansq + 1e-05) * gain.reshape(1, GROUPS, -1)
    return scaled.reshape(row_count, -1).astype(jnp.bfloat16)

def one_sequence(token_rows, rates, conv_weight, conv_bias, dt_bias, a_log, skip, norm_gain):
    length = token_rows.shape[0]
    inner_width = HEADS * P_SIZE
    per_group = HEADS // GROUPS
    padded = jnp.concatenate([jnp.zeros((3, token_rows.shape[1]), jnp.bfloat16), token_rows], axis=0)
    conv_out = conv_silu(padded, conv_weight, conv_bias)
    values = conv_out[:, :inner_width].reshape(length, GROUPS, per_group, P_SIZE)
    keys_in = conv_out[:, inner_width:inner_width + GROUPS * N].reshape(length, GROUPS, N)
    queries = conv_out[:, inner_width + GROUPS * N:].reshape(length, GROUPS, N)
    delta = jax.nn.softplus(rates.astype(jnp.float32) + dt_bias[None, :]).reshape(length, GROUPS, per_group)
    decay = -jnp.exp(a_log).reshape(1, GROUPS, per_group) * delta
    state = jnp.zeros((GROUPS, per_group, P_SIZE, N), jnp.float32)
    swept = span_sweep(values, keys_in, queries, delta, decay, state, min(64, length))
    outputs = swept[0] + skip.reshape(1, GROUPS, per_group, 1) * values.astype(jnp.float32)
    return group_norm(outputs.reshape(length, inner_width).astype(jnp.bfloat16), norm_gain)

def reference(xbc, dt, conv_weight, conv_bias, dt_bias, a_log, skip, norm_gain):
    return one_sequence(xbc, dt, conv_weight, conv_bias, dt_bias, a_log, skip, norm_gain)
```

```python
import functools

import jax
import jax.numpy as jnp
from jax import lax
from jax.experimental import pallas as pl
from jax.experimental.pallas import tpu as pltpu
from jax.sharding import PartitionSpec as P

P_SIZE = 64
N = 128
GROUPS = 4
HALO = 16
CHUNKS = 4
F32, BF16 = jnp.float32, jnp.bfloat16
ANY = pl.BlockSpec(memory_space=pl.ANY)
VM = pl.BlockSpec(memory_space=pltpu.VMEM)


def place():
    f, c = lax.axis_index("fsdp"), lax.axis_index("ctx")
    nz = lax.axis_size("ctx") // GROUPS
    nf = lax.axis_size("fsdp")
    g, z = lax.rem(c, GROUPS), c // GROUPS
    return f, c, g, z, nz, nf, f * nz + z


def device(seg, g, nz):
    return {"fsdp": seg // nz, "ctx": lax.rem(seg, nz) * GROUPS + g}


def lanes(index, size):
    return pl.ds(pl.multiple_of(index * size, 128), size)


def gather_kernel(x, dt, cw, cb, gn, sm, xo, bc, dto, halo, cwo, cbo, gno, smo,
                  send, recv, psend, precv, hsend, hrecv, own_sem):
    f, c, g, z, nz, nf, seg = place()
    last = nz * nf - 1
    gw = xo.shape[2]
    di = gw * GROUPS
    barrier = pltpu.get_barrier_semaphore()
    for d in range(1, GROUPS):
        peer = lax.rem(g + d, GROUPS)
        pl.semaphore_signal(barrier, inc=1, device_id={"fsdp": f, "ctx": z * GROUPS + peer})
    for d in range(1, nf):
        pl.semaphore_signal(barrier, inc=1, device_id={"fsdp": lax.rem(f + d, nf), "ctx": c})

    @pl.when(seg > 0)
    def _():
        pl.semaphore_signal(barrier, inc=1, device_id=device(seg - 1, GROUPS - 1, nz))

    sends_halo = jnp.logical_and(g == GROUPS - 1, seg < last)
    pl.semaphore_wait(barrier, GROUPS - 1 + nf - 1 + jnp.where(sends_halo, GROUPS, 0))

    def pieces(p, rows, to):
        return [
            (x.at[rows, lanes(p, gw)], to[0]),
            (x.at[rows, pl.ds(pl.multiple_of(di + p * N, 128), N)], to[1]),
            (x.at[rows, pl.ds(pl.multiple_of(di + (GROUPS + p) * N, 128), N)], to[2]),
        ]

    def halo_copies():
        out = []
        for p in range(GROUPS):
            to = [halo.at[:, 0:gw], halo.at[:, gw : gw + N], halo.at[:, gw + N : gw + 2 * N]]
            rows = pl.ds(x.shape[0] - HALO, HALO)
            for k, (src, dst) in enumerate(pieces(p, rows, to)):
                out.append(pltpu.make_async_remote_copy(
                    src, dst, hsend.at[p, k], hrecv.at[k],
                    device_id=device(seg + 1, p, nz)))
        return out

    @pl.when(sends_halo)
    def _():
        for copy in halo_copies():
            copy.start()

    rows = pl.ds(0, x.shape[0])
    to = [xo.at[g], bc.at[g, :, 0:N], bc.at[g, :, N : 2 * N]]
    copies = []
    for d in (2, 1, 3):
        p = lax.rem(g + d, GROUPS)
        parts = pieces(p, rows, to) + [(dt, dto.at[g])]
        for k, (src, dst) in enumerate(parts):
            copies.append(pltpu.make_async_remote_copy(
                src, dst, send.at[d, k], recv.at[d, k],
                device_id={"fsdp": f, "ctx": z * GROUPS + p}))
    params = [
        (cw, cwo.at[:, lanes(f, cw.shape[1])]),
        (cb, cbo.at[:, lanes(f, cb.shape[1])]),
        (gn, gno.at[:, lanes(f, gn.shape[1])]),
        (sm, smo.at[f]),
    ]
    for d in range(1, nf):
        for k, (src, dst) in enumerate(params):
            copies.append(pltpu.make_async_remote_copy(
                src, dst, psend.at[d, k], precv.at[d, k],
                device_id={"fsdp": lax.rem(f + d, nf), "ctx": c}))
    for copy in copies:
        copy.start()
    owns = [pltpu.make_async_copy(src, dst, own_sem.at[k])
            for k, (src, dst) in enumerate(pieces(g, rows, to) + [(dt, dto.at[g])] + params)]
    for copy in owns:
        copy.start()
    for copy in owns:
        copy.wait()
    for copy in copies:
        copy.wait()

    @pl.when(sends_halo)
    def _():
        for copy in halo_copies():
            copy.wait_send()

    @pl.when(seg > 0)
    def _():
        for copy in halo_copies()[:3]:
            copy.wait_recv()


def gather(x, dt, cw, cb, gn, sm):
    rows, ch = x.shape
    nf = lax.axis_size("fsdp")
    gw = dt.shape[1] * P_SIZE // GROUPS
    sds = jax.ShapeDtypeStruct
    dma = pltpu.SemaphoreType.DMA
    return pl.pallas_call(
        gather_kernel,
        out_shape=(
            sds((GROUPS, rows, gw), BF16),
            sds((GROUPS, rows, 2 * N), BF16),
            sds((GROUPS,) + dt.shape, BF16),
            sds((HALO, gw + 2 * N), BF16),
            sds((4, ch), F32),
            sds((1, ch), F32),
            sds((1, gw * GROUPS), F32),
            sds((nf,) + sm.shape, F32),
        ),
        in_specs=[ANY] * 6,
        out_specs=(ANY,) * 8,
        scratch_shapes=[dma((GROUPS, 4)), dma((GROUPS, 4)), dma((nf, 4)), dma((nf, 4)),
                        dma((GROUPS, 3)), dma((3,)), dma((8,))],
        compiler_params=pltpu.CompilerParams(collective_id=0, has_side_effects=True),
        name="gather",
    )(x, dt, cw, cb, gn, sm)


def hi_lo(v):
    hi = v.astype(BF16)
    return jnp.concatenate([hi, (v - hi.astype(F32)).astype(BF16)], axis=1)


def dot(a, b, dims=((1,), (0,))):
    return lax.dot_general(a, b, (dims, ((), ())), preferred_element_type=F32)


def fill_selection(sel, g):
    heads, width = sel.shape[0] // 2, sel.shape[1]
    per_group = width // P_SIZE
    row = lax.broadcasted_iota(jnp.int32, sel.shape, 0)
    col = lax.broadcasted_iota(jnp.int32, sel.shape, 1)
    row = jnp.where(row >= heads, row - heads, row)
    sel[...] = jnp.where(row == g * per_group + col // P_SIZE, 1.0, 0.0).astype(BF16)


def local_kernel(x, bc, dt, halo, cw, cb, sm, zo, co, ao, po, do,
                 ext, act, sel, state, decayed):
    _, _, g, _, _, _, seg = place()
    j = pl.program_id(0)
    rows, gw = x.shape[1], x.shape[2]
    di = gw * GROUPS
    width = 256
    bases = [(g * gw, gw), (di + g * N, N), (di + (GROUPS + g) * N, N)]

    @pl.when(j == 0)
    def _():
        fill_selection(sel, g)
        ext[0:8, :] = jnp.where(seg > 0, halo[HALO - 8 :, :].astype(F32), 0.0)
        state[...] = jnp.zeros_like(state)
        decayed[...] = jnp.ones_like(decayed)

    @pl.when(j > 0)
    def _():
        ext[0:8, :] = ext[rows : rows + 8, :]

    ext[8 : 8 + rows, 0:gw] = x[0].astype(F32)
    ext[8 : 8 + rows, gw:] = bc[0].astype(F32)

    def conv(src, dst, size):
        here = pl.ds(src, size)
        total = cb[0:1, pl.ds(dst, size)] + cw[0:1, pl.ds(dst, size)] * ext[5 : 5 + rows, here]
        for k in range(1, 4):
            total = total + cw[k : k + 1, pl.ds(dst, size)] * ext[5 + k : 5 + k + rows, here]
        act[:, here] = (total / (1.0 + jnp.exp(-total))).astype(BF16)

    @pl.loop(0, gw // width)
    def _(i):
        conv(pl.multiple_of(i * width, width), pl.multiple_of(bases[0][0] + i * width, 128), width)

    conv(gw, pl.multiple_of(bases[1][0], 128), N)
    conv(gw + N, pl.multiple_of(bases[2][0], 128), N)

    vectors = sm[0]
    for f in range(1, sm.shape[0]):
        vectors = vectors + sm[f]
    delta = dt[0].astype(F32) + vectors[0:1, :]
    delta = jnp.maximum(delta, 0.0) + jnp.log1p(jnp.exp(-jnp.abs(delta)))
    rate = -jnp.exp(vectors[1:2, :]) * delta
    lower = (lax.broadcasted_iota(jnp.int32, (rows, rows), 0)
             >= lax.broadcasted_iota(jnp.int32, (rows, rows), 1))
    cum = lax.dot_general(jnp.where(lower, 1.0, 0.0), rate, (((1,), (0,)), ((), ())),
                          precision=lax.Precision.HIGHEST, preferred_element_type=F32)
    decay = jnp.exp(cum)
    source = hi_lo(delta * jnp.exp(-cum))
    block_decay = decay[rows - 1 : rows, :]
    ao[0] = hi_lo(decay * decayed[0:1, :])
    decay_2 = hi_lo(decay)
    vec_2 = hi_lo(jnp.concatenate(
        [vectors[2:3, :], block_decay, decayed[0:1, :] * block_decay, vectors[3:8, :]], axis=0))
    decayed[...] = decayed[...] * block_decay
    keys, queries = act[:, gw : gw + N], act[:, gw + N : gw + 2 * N]
    scores = jnp.where(lower, dot(queries, keys, ((1,), (1,))), 0.0).astype(BF16)
    left = jnp.concatenate([scores, queries], axis=1)
    co[0] = queries
    part = 512

    @pl.loop(0, gw // part)
    def _(i):
        here = lanes(i, part)
        pick = sel[:, here]
        values = act[:, here].astype(F32)
        weighted = (values * dot(source, pick)).astype(BF16)
        vec = dot(vec_2, pick)
        old = state[:, here]
        inner = dot(left, jnp.concatenate([weighted, old.astype(BF16)], axis=0))
        zo[0, :, here] = dot(decay_2, pick) * inner + vec[0:1, :] * values
        new = vec[1:2, :] * (old + dot(keys, weighted, ((0,), (0,))))
        state[:, here] = new
        po[:, here] = new
        do[:, here] = jnp.broadcast_to(vec[2:3, :], (8, part))


def local_part(x, bc, dt, halo, cw, cb, sm):
    blocks, rows, gw = x.shape
    heads = dt.shape[2]
    sds = jax.ShapeDtypeStruct

    def block(shape):
        return pl.BlockSpec((1,) + shape, lambda j: (j, 0, 0))

    def whole(array):
        return pl.BlockSpec(array, lambda j: (0,) * len(array))

    return pl.pallas_call(
        local_kernel,
        grid=(blocks,),
        out_shape=(sds((blocks, rows, gw), F32), sds((blocks, rows, N), BF16),
                   sds((blocks, rows, 2 * heads), BF16), sds((N, gw), F32), sds((8, gw), F32)),
        in_specs=[block((rows, gw)), block((rows, 2 * N)), block((rows, heads)),
                  whole(halo.shape), whole(cw.shape), whole(cb.shape), whole(sm.shape)],
        out_specs=(block((rows, gw)), block((rows, N)), block((rows, 2 * heads)),
                   whole((N, gw)), whole((8, gw))),
        scratch_shapes=[pltpu.VMEM((8 + rows, gw + 2 * N), F32),
                        pltpu.VMEM((rows, gw + 2 * N), BF16),
                        pltpu.VMEM((2 * heads, gw), BF16),
                        pltpu.VMEM((N, gw), F32),
                        pltpu.VMEM((8, heads), F32)],
        compiler_params=pltpu.CompilerParams(vmem_limit_bytes=40 << 20),
        name="local_part",
    )(x, bc, dt, halo, cw, cb, sm)


def chain_kernel(z_hbm, queries, decays, own_state, own_decay, gain, out,
                 z_buf, q_buf, r_buf, q_low, o_buf, sel,
                 csend, crecv, osend, orecv, z_sem, own_sem):
    f, c, g, z, nz, nf, seg = place()
    last = nz * nf - 1
    gw = own_state.shape[1]
    part = gw // CHUNKS
    load = pltpu.make_async_copy(z_hbm, z_buf, z_sem)
    load.start()
    barrier = pltpu.get_barrier_semaphore()
    for d in range(1, GROUPS):
        peer = lax.rem(g + d, GROUPS)
        pl.semaphore_signal(barrier, inc=1, device_id={"fsdp": f, "ctx": z * GROUPS + peer})

    @pl.when(seg > 0)
    def _():
        pl.semaphore_signal(barrier, inc=1, device_id=device(seg - 1, g, nz))

    @pl.when(seg == 0)
    def _():
        q_buf[...] = jnp.zeros_like(q_buf)

    fill_selection(sel, g)
    pl.semaphore_wait(barrier, GROUPS - 1 + jnp.where(seg < last, 1, 0))

    def hop(i):
        return pltpu.make_async_remote_copy(
            r_buf.at[i], q_buf.at[i], csend.at[i], crecv.at[i],
            device_id=device(seg + 1, g, nz))

    @pl.loop(0, CHUNKS)
    def _(i):
        here = lanes(i, part)

        @pl.when(seg > 0)
        def _():
            hop(i).wait_recv()

        state = q_buf[i]

        @pl.when(seg < last)
        def _():
            r_buf[i] = own_state[:, here] + own_decay[0:1, here] * state
            hop(i).start()

        q_low[:, here] = state.astype(BF16)

    load.wait()
    mine = lanes(g, gw)

    def finish(j):
        total = jnp.zeros((z_buf.shape[1], 1), F32)
        for i in range(CHUNKS):
            here = pl.ds(i * part, part)
            carried = dot(queries[j], q_low[:, here]) * dot(decays[j], sel[:, here])
            y = (z_buf[j, :, here] + carried).astype(BF16)
            o_buf[j, :, here] = y
            y = y.astype(F32)
            total = total + jnp.sum(y * y, axis=1, keepdims=True)
        scale = lax.rsqrt(total * (1.0 / gw) + 1e-05)
        for i in range(CHUNKS):
            here = pl.ds(i * part, part)
            y = o_buf[j, :, here].astype(F32) * scale * gain[0:1, lanes(g * CHUNKS + i, part)]
            o_buf[j, :, here] = y.astype(BF16)

    def back(d):
        j = lax.rem(g + d, GROUPS)
        return pltpu.make_async_remote_copy(
            o_buf.at[j], out.at[:, mine], osend.at[d], orecv.at[d],
            device_id={"fsdp": f, "ctx": z * GROUPS + j})

    @pl.loop(1, GROUPS)
    def _(d):
        finish(lax.rem(g + d, GROUPS))
        back(d).start()

    finish(g)
    own = pltpu.make_async_copy(o_buf.at[g], out.at[:, mine], own_sem)
    own.start()

    @pl.when(seg < last)
    def _():
        for i in range(CHUNKS):
            hop(i).wait_send()

    own.wait()
    for d in range(1, GROUPS):
        back(d).wait()


def chain(z_part, queries, decays, own_state, own_decay, gain):
    blocks, rows, gw = z_part.shape
    dma = pltpu.SemaphoreType.DMA
    part = gw // CHUNKS
    return pl.pallas_call(
        chain_kernel,
        out_shape=jax.ShapeDtypeStruct((rows, gw * GROUPS), BF16),
        in_specs=[ANY, VM, VM, VM, VM, VM],
        out_specs=ANY,
        scratch_shapes=[pltpu.VMEM(z_part.shape, F32),
                        pltpu.VMEM((CHUNKS, N, part), F32),
                        pltpu.VMEM((CHUNKS, N, part), F32),
                        pltpu.VMEM((N, gw), BF16),
                        pltpu.VMEM((blocks, rows, gw), BF16),
                        pltpu.VMEM((decays.shape[2], gw), BF16),
                        dma((CHUNKS,)), dma((CHUNKS,)), dma((GROUPS,)), dma((GROUPS,)),
                        dma, dma],
        compiler_params=pltpu.CompilerParams(
            collective_id=1, has_side_effects=True, vmem_limit_bytes=40 << 20),
        name="chain",
    )(z_part, queries, decays, own_state, own_decay, gain)


def local(xbc, dt, conv_weight, conv_bias, dt_bias, a_log, skip, norm_gain):
    heads = dt.shape[1]
    own = dt_bias.shape[0]
    small = jnp.stack([dt_bias, a_log, skip])
    small = lax.dynamic_update_slice(
        jnp.zeros((8, heads), F32), small, (0, lax.axis_index("fsdp") * own))
    x, bc, rates, halo, cw, cb, gain, sm = gather(
        xbc, dt, conv_weight, conv_bias[None], norm_gain[None], small)
    z_part, queries, decays, state, decay = local_part(x, bc, rates, halo, cw, cb, sm)
    return chain(z_part, queries, decays, state, decay, gain)


def solution(mesh):
    placed = (
        P(("fsdp", "ctx"), None),
        P(("fsdp", "ctx"), None),
        P(None, "fsdp"),
        P("fsdp"),
        P("fsdp"),
        P("fsdp"),
        P("fsdp"),
        P("fsdp"),
    )
    return jax.shard_map(
        local, mesh=mesh, in_specs=placed, out_specs=P(("fsdp", "ctx"), None), check_vma=False
    )
```

```python
import jax
import jax.numpy as jnp
from jax import lax
from jax.experimental import pallas as pl
from jax.experimental.pallas import tpu as pltpu
from jax.sharding import PartitionSpec as P

P_SIZE = 64
N = 128
GROUPS = 4
HALO = 16
WIDTH = 256
F32, BF16 = jnp.float32, jnp.bfloat16
ANY = pl.BlockSpec(memory_space=pl.ANY)


def place():
    f, c = lax.axis_index("fsdp"), lax.axis_index("ctx")
    nz = lax.axis_size("ctx") // GROUPS
    nf = lax.axis_size("fsdp")
    g, z = lax.rem(c, GROUPS), c // GROUPS
    return f, c, g, z, nz, nf, f * nz + z


def device(seg, g, nz):
    return {"fsdp": seg // nz, "ctx": lax.rem(seg, nz) * GROUPS + g}


def lanes(index, size):
    return pl.ds(pl.multiple_of(index * size, 128), size)


def hi_lo(v):
    hi = v.astype(BF16)
    return jnp.concatenate([hi, (v - hi.astype(F32)).astype(BF16)], axis=1)


def dot(a, b, dims=((1,), (0,))):
    return lax.dot_general(a, b, (dims, ((), ())), preferred_element_type=F32)


def fill_selection(sel, g):
    heads, width = sel.shape[0] // 2, sel.shape[1]
    per_group = width // P_SIZE
    row = lax.broadcasted_iota(jnp.int32, sel.shape, 0)
    col = lax.broadcasted_iota(jnp.int32, sel.shape, 1)
    row = jnp.where(row >= heads, row - heads, row)
    sel[...] = jnp.where(row == g * per_group + col // P_SIZE, 1.0, 0.0).astype(BF16)


def silu_conv(ext, start, cw, at, size):
    rows = ext.shape[0] - 8
    total = cw[4:5, at]
    for k in range(4):
        total = total + cw[k : k + 1, at] * ext[5 + k : 5 + k + rows, start : start + size]
    return (total / (1.0 + jnp.exp(-total))).astype(BF16)


def mixer_kernel(x, dt, cw_in, gn_in, out,
                 raw, raw_bc, dts, halo, cw, gn, sel, ext, keys, left, source, decay_2, carry_2,
                 vec_2, z_buf, p_buf, q_buf, r_buf, y_out, y_in, o_buf,
                 xsend, xrecv, bsend, brecv, psend, precv, hsend, hrecv, csend, crecv,
                 osend, orecv, xown, own_sem, out_sem):
    f, c, g, z, nz, nf, seg = place()
    last = nz * nf - 1
    rows = x.shape[0]
    chunks = raw.shape[0]
    gw = chunks * WIDTH
    di = gw * GROUPS
    heads = dt.shape[1]

    def peer(d):
        return {"fsdp": f, "ctx": z * GROUPS + lax.rem(g + d, GROUPS)}

    def sibling(d):
        return {"fsdp": lax.rem(f + d, nf), "ctx": c}

    barrier = pltpu.get_barrier_semaphore()
    for d in range(1, GROUPS):
        pl.semaphore_signal(barrier, inc=1, device_id=peer(d))
    for d in range(1, nf):
        pl.semaphore_signal(barrier, inc=1, device_id=sibling(d))

    @pl.when(seg > 0)
    def _():
        pl.semaphore_signal(barrier, inc=1, device_id=device(seg - 1, g, nz))

    @pl.when(jnp.logical_and(seg > 0, g < GROUPS - 1))
    def _():
        pl.semaphore_signal(barrier, inc=1, device_id=device(seg - 1, GROUPS - 1, nz))

    more = jnp.where(seg < last, jnp.where(g == GROUPS - 1, GROUPS, 1), 0)
    pl.semaphore_wait(barrier, GROUPS - 1 + nf - 1 + more)

    def b_at(p):
        return pl.ds(pl.multiple_of(di + p * N, 128), N)

    def c_at(p):
        return pl.ds(pl.multiple_of(di + (GROUPS + p) * N, 128), N)

    mine = pl.ds(pl.multiple_of(g * rows, 128), rows)

    def halo_copies():
        out = []
        tail = pl.ds(rows - HALO, HALO)
        for p in range(GROUPS):
            parts = [(x.at[tail, lanes(p, gw)], halo.at[:, 0:gw]),
                     (x.at[tail, b_at(p)], halo.at[:, gw : gw + N]),
                     (x.at[tail, c_at(p)], halo.at[:, gw + N : gw + 2 * N])]
            for k, (src, dst) in enumerate(parts):
                out.append(pltpu.make_async_remote_copy(
                    src, dst, hsend.at[p, k], hrecv.at[k], device_id=device(seg + 1, p, nz)))
        return out

    sends_halo = jnp.logical_and(g == GROUPS - 1, seg < last)

    @pl.when(sends_halo)
    def _():
        for copy in halo_copies():
            copy.start()

    params = [(cw_in, cw.at[:, lanes(f, cw_in.shape[1])]), (gn_in, gn.at[:, lanes(f, gn_in.shape[1])])]

    def small(p):
        return [(x.at[:, b_at(p)], raw_bc.at[mine, 0:N]),
                (x.at[:, c_at(p)], raw_bc.at[mine, N : 2 * N]), (dt, dts.at[g])]

    first = []
    for d in range(1, nf):
        for k, (src, dst) in enumerate(params):
            first.append(pltpu.make_async_remote_copy(
                src, dst, psend.at[d, k], precv.at[d, k], device_id=sibling(d)))
    for d in (2, 1, 3):
        for k, (src, dst) in enumerate(small(lax.rem(g + d, GROUPS))):
            first.append(pltpu.make_async_remote_copy(
                src, dst, bsend.at[d, k], brecv.at[d, k], device_id=peer(d)))
    for k, (src, dst) in enumerate(small(g) + params):
        first.append(pltpu.make_async_copy(src, dst, own_sem.at[k]))
    for copy in first:
        copy.start()

    def pieces(q):
        out = []
        for d in (2, 1, 3):
            p = lax.rem(g + d, GROUPS)
            out.append(pltpu.make_async_remote_copy(
                x.at[:, lanes(p * chunks + q, WIDTH)], raw.at[q, mine], xsend.at[d, q],
                xrecv.at[d, q], device_id=peer(d)))
        out.append(pltpu.make_async_copy(
            x.at[:, lanes(g * chunks + q, WIDTH)], raw.at[q, mine], xown.at[q]))
        return out

    @pl.loop(0, chunks)
    def _(q):
        for copy in pieces(q):
            copy.start()

    @pl.when(seg == 0)
    def _():
        q_buf[...] = jnp.zeros_like(q_buf)

    fill_selection(sel, g)
    for copy in first:
        copy.wait()

    @pl.when(seg > 0)
    def _():
        for copy in halo_copies()[:3]:
            copy.wait_recv()

    def before(at, size):
        return jnp.where(seg > 0, halo[HALO - 8 :, at].astype(F32), 0.0)

    ext[0:8, :] = before(pl.ds(gw, 2 * N), 2 * N)
    ext[8:, :] = raw_bc[...].astype(F32)
    keys[...] = silu_conv(ext, 0, cw, b_at(g), N)
    queries = silu_conv(ext, N, cw, c_at(g), N)
    vectors = cw[5:8, 0:heads]
    for d in range(1, nf):
        vectors = vectors + cw[5:8, pl.ds(d * cw_in.shape[1], heads)]
    lower = (lax.broadcasted_iota(jnp.int32, (rows, rows), 0)
             >= lax.broadcasted_iota(jnp.int32, (rows, rows), 1))
    ones = jnp.where(lower, 1.0, 0.0)
    scale = jnp.exp(vectors[1:2, :])
    decayed = jnp.ones((1, heads), F32)
    for j in range(GROUPS):
        at = pl.ds(j * rows, rows)
        delta = dts[j].astype(F32) + vectors[0:1, :]
        delta = jnp.maximum(delta, 0.0) + jnp.log1p(jnp.exp(-jnp.abs(delta)))
        cum = lax.dot_general(ones, -scale * delta, (((1,), (0,)), ((), ())),
                              precision=lax.Precision.HIGHEST, preferred_element_type=F32)
        decay = jnp.exp(cum)
        source[j] = hi_lo(delta * jnp.exp(-cum))
        decay_2[j] = hi_lo(decay)
        carry_2[j] = hi_lo(decay * decayed)
        block_decay = decay[rows - 1 : rows, :]
        decayed = decayed * block_decay
        vec_2[j] = hi_lo(jnp.concatenate(
            [vectors[2:3, :], block_decay, decayed, jnp.zeros((5, heads), F32)], axis=0))
        mine_q = queries[j * rows : (j + 1) * rows]
        scores = jnp.where(lower, dot(mine_q, keys[at, :], ((1,), (1,))), 0.0).astype(BF16)
        left[j] = jnp.concatenate([scores, mine_q], axis=1)

    def local_step(q):
        for copy in pieces(q)[:3]:
            copy.wait_recv()
        pieces(q)[3].wait()
        here = lanes(q, WIDTH)
        ext[0:8, :] = before(here, WIDTH)
        ext[8:, :] = raw[q].astype(F32)
        act = silu_conv(ext, 0, cw, lanes(g * chunks + q, WIDTH), WIDTH)
        pick = sel[:, here]
        state = jnp.zeros((N, WIDTH), F32)
        for j in range(GROUPS):
            values = act[j * rows : (j + 1) * rows].astype(F32)
            weighted = (values * dot(source[j], pick)).astype(BF16)
            vec = dot(vec_2[j], pick)
            inner = dot(left[j], jnp.concatenate([weighted, state.astype(BF16)], axis=0))
            z_buf[q, j] = dot(decay_2[j], pick) * inner + vec[0:1, :] * values
            state = vec[1:2, :] * (state + dot(keys[pl.ds(j * rows, rows), :], weighted, ((0,), (0,))))
        p_buf[q] = state

    def hop(q):
        return pltpu.make_async_remote_copy(
            r_buf.at[q], q_buf.at[q], csend.at[q], crecv.at[q], device_id=device(seg + 1, g, nz))

    def back(d, q):
        return pltpu.make_async_remote_copy(
            y_out.at[lax.rem(g + d, GROUPS), q], y_in.at[g, q], osend.at[d, q], orecv.at[d, q],
            device_id=peer(d))

    def carry_step(q):
        pick = sel[:, lanes(q, WIDTH)]

        @pl.when(seg > 0)
        def _():
            hop(q).wait_recv()

        state = q_buf[q]

        @pl.when(seg < last)
        def _():
            through = dot(vec_2[GROUPS - 1], pick)[2:3, :]
            r_buf[q] = (p_buf[q] + through * state.astype(F32)).astype(r_buf.dtype)
            hop(q).start()

        low = state.astype(BF16)
        for j in range(GROUPS):
            carried = dot(left[j, :, N:], low) * dot(carry_2[j], pick)
            y_out[j, q] = (z_buf[q, j] + carried).astype(BF16)
        for d in range(1, GROUPS):
            back(d, q).start()
        y_in[g, q] = y_out[g, q]

    lag = seg if nz * nf <= chunks else jnp.where(seg < chunks, seg, chunks)

    @pl.loop(0, 2 * chunks)
    def _(i):
        @pl.when(i < chunks)
        def _():
            local_step(i)

        @pl.when(jnp.logical_and(i >= lag, i < lag + chunks))
        def _():
            carry_step(i - lag)

    @pl.loop(0, chunks)
    def _(q):
        for copy in pieces(q)[:3]:
            copy.wait_send()
        for d in range(1, GROUPS):
            back(d, q).wait()

    def finished(p):
        at = lanes(p, gw)
        return pltpu.make_async_copy(o_buf.at[:, at], out.at[:, at], out_sem.at[p])

    @pl.loop(0, GROUPS)
    def _(p):
        total = jnp.zeros((rows, WIDTH), F32)
        for q in range(chunks):
            y = y_in[p, q].astype(F32)
            total = total + y * y
        norm = lax.rsqrt(jnp.sum(total, axis=1, keepdims=True) * (1.0 / gw) + 1e-05)
        for q in range(chunks):
            at = lanes(p * chunks + q, WIDTH)
            o_buf[:, at] = (y_in[p, q].astype(F32) * norm * gn[0:1, at]).astype(BF16)
        finished(p).start()

    @pl.when(seg < last)
    def _():
        @pl.loop(0, chunks)
        def _(q):
            hop(q).wait_send()

    @pl.when(sends_halo)
    def _():
        for copy in halo_copies():
            copy.wait_send()

    for p in range(GROUPS):
        finished(p).wait()


def mixer(x, dt, cw, gn):
    rows, ch = x.shape
    heads = dt.shape[1]
    nf = lax.axis_size("fsdp")
    segments = nf * (lax.axis_size("ctx") // GROUPS)
    gw = heads * P_SIZE // GROUPS
    chunks = gw // WIDTH
    length = rows * GROUPS
    link = BF16 if segments <= 8 else F32
    vm, dma = pltpu.VMEM, pltpu.SemaphoreType.DMA
    return pl.pallas_call(
        mixer_kernel,
        out_shape=jax.ShapeDtypeStruct((rows, gw * GROUPS), BF16),
        in_specs=[ANY] * 4,
        out_specs=ANY,
        scratch_shapes=[
            vm((chunks, length, WIDTH), BF16),
            vm((length, 2 * N), BF16),
            vm((GROUPS, rows, heads), BF16),
            vm((HALO, gw + 2 * N), BF16),
            vm((8, ch), F32),
            vm((1, gw * GROUPS), F32),
            vm((2 * heads, gw), BF16),
            vm((8 + length, WIDTH), F32),
            vm((length, N), BF16),
            vm((GROUPS, rows, 2 * N), BF16),
            vm((GROUPS, rows, 2 * heads), BF16),
            vm((GROUPS, rows, 2 * heads), BF16),
            vm((GROUPS, rows, 2 * heads), BF16),
            vm((GROUPS, 8, 2 * heads), BF16),
            vm((chunks, GROUPS, rows, WIDTH), F32),
            vm((chunks, N, WIDTH), F32),
            vm((chunks, N, WIDTH), link),
            vm((chunks, N, WIDTH), link),
            vm((GROUPS, chunks, rows, WIDTH), BF16),
            vm((GROUPS, chunks, rows, WIDTH), BF16),
            vm((rows, gw * GROUPS), BF16),
            dma((GROUPS, chunks)), dma((GROUPS, chunks)), dma((GROUPS, 3)), dma((GROUPS, 3)),
            dma((nf, 2)), dma((nf, 2)), dma((GROUPS, 3)), dma((3,)),
            dma((chunks,)), dma((chunks,)), dma((GROUPS, chunks)), dma((GROUPS, chunks)),
            dma((chunks,)), dma((5,)), dma((GROUPS,)),
        ],
        compiler_params=pltpu.CompilerParams(
            collective_id=0, has_side_effects=True, vmem_limit_bytes=48 << 20),
        name="mixer",
    )(x, dt, cw, gn)


def local(xbc, dt, conv_weight, conv_bias, dt_bias, a_log, skip, norm_gain):
    heads = dt.shape[1]
    own = dt_bias.shape[0]
    width = conv_bias.shape[0]
    small = lax.dynamic_update_slice(
        jnp.zeros((3, width), F32), jnp.stack([dt_bias, a_log, skip]),
        (0, lax.axis_index("fsdp") * own))
    params = jnp.concatenate([conv_weight, conv_bias[None], small], axis=0)
    return mixer(xbc, dt, params, norm_gain[None])


def solution(mesh):
    placed = (
        P(("fsdp", "ctx"), None),
        P(("fsdp", "ctx"), None),
        P(None, "fsdp"),
        P("fsdp"),
        P("fsdp"),
        P("fsdp"),
        P("fsdp"),
        P("fsdp"),
    )
    return jax.shard_map(
        local, mesh=mesh, in_specs=placed, out_specs=P(("fsdp", "ctx"), None), check_vma=False
    )
```

```python
import jax
import jax.numpy as jnp
from jax import lax
from jax.experimental import pallas as pl
from jax.experimental.pallas import tpu as pltpu
from jax.sharding import PartitionSpec as P

P_SIZE = 64
N = 128
GROUPS = 4
HALO = 16
WIDTH = 256
F32, BF16 = jnp.float32, jnp.bfloat16
ANY = pl.BlockSpec(memory_space=pl.ANY)


def place():
    f, c = lax.axis_index("fsdp"), lax.axis_index("ctx")
    nz = lax.axis_size("ctx") // GROUPS
    nf = lax.axis_size("fsdp")
    g, z = lax.rem(c, GROUPS), c // GROUPS
    return f, c, g, z, nz, nf, f * nz + z


def device(seg, g, nz):
    return {"fsdp": seg // nz, "ctx": lax.rem(seg, nz) * GROUPS + g}


def lanes(index, size):
    return pl.ds(pl.multiple_of(index * size, 128), size)


def hi_lo(v):
    hi = v.astype(BF16)
    return jnp.concatenate([hi, (v - hi.astype(F32)).astype(BF16)], axis=1)


def dot(a, b, dims=((1,), (0,))):
    return lax.dot_general(a, b, (dims, ((), ())), preferred_element_type=F32)


def fill_selection(sel, g):
    heads, width = sel.shape[0] // 2, sel.shape[1]
    per_group = width // P_SIZE
    row = lax.broadcasted_iota(jnp.int32, sel.shape, 0)
    col = lax.broadcasted_iota(jnp.int32, sel.shape, 1)
    row = jnp.where(row >= heads, row - heads, row)
    sel[...] = jnp.where(row == g * per_group + col // P_SIZE, 1.0, 0.0).astype(BF16)


def silu_conv(ext, start, cw, at, size):
    rows = ext.shape[0] - 8
    total = cw[4:5, at]
    for k in range(4):
        total = total + cw[k : k + 1, at] * ext[5 + k : 5 + k + rows, start : start + size]
    return (total / (1.0 + jnp.exp(-total))).astype(BF16)


def mixer_kernel(x, dt, cw_in, gn_in, out,
                 raw, raw_bc, dts, halo, cw, gn, sel, ext, keys, left, source, decay_2, carry_2,
                 vec_2, z_buf, p_buf, q_buf, r_buf, y_out, y_in, o_buf, squares,
                 xsend, xrecv, bsend, brecv, psend, precv, hsend, hrecv, csend, crecv,
                 osend, orecv, xown, own_sem, out_sem):
    f, c, g, z, nz, nf, seg = place()
    last = nz * nf - 1
    rows = x.shape[0]
    chunks = raw.shape[0]
    gw = chunks * WIDTH
    di = gw * GROUPS
    heads = dt.shape[1]

    def peer(d):
        return {"fsdp": f, "ctx": z * GROUPS + lax.rem(g + d, GROUPS)}

    def sibling(d):
        return {"fsdp": lax.rem(f + d, nf), "ctx": c}

    barrier = pltpu.get_barrier_semaphore()
    for d in range(1, GROUPS):
        pl.semaphore_signal(barrier, inc=1, device_id=peer(d))
    for d in range(1, nf):
        pl.semaphore_signal(barrier, inc=1, device_id=sibling(d))

    @pl.when(seg > 0)
    def _():
        pl.semaphore_signal(barrier, inc=1, device_id=device(seg - 1, g, nz))

    @pl.when(jnp.logical_and(seg > 0, g < GROUPS - 1))
    def _():
        pl.semaphore_signal(barrier, inc=1, device_id=device(seg - 1, GROUPS - 1, nz))

    more = jnp.where(seg < last, jnp.where(g == GROUPS - 1, GROUPS, 1), 0)
    pl.semaphore_wait(barrier, GROUPS - 1 + nf - 1 + more)

    def b_at(p):
        return pl.ds(pl.multiple_of(di + p * N, 128), N)

    def c_at(p):
        return pl.ds(pl.multiple_of(di + (GROUPS + p) * N, 128), N)

    mine = pl.ds(pl.multiple_of(g * rows, 128), rows)

    def halo_copies():
        out = []
        tail = pl.ds(rows - HALO, HALO)
        for p in range(GROUPS):
            parts = [(x.at[tail, lanes(p, gw)], halo.at[:, 0:gw]),
                     (x.at[tail, b_at(p)], halo.at[:, gw : gw + N]),
                     (x.at[tail, c_at(p)], halo.at[:, gw + N : gw + 2 * N])]
            for k, (src, dst) in enumerate(parts):
                out.append(pltpu.make_async_remote_copy(
                    src, dst, hsend.at[p, k], hrecv.at[k], device_id=device(seg + 1, p, nz)))
        return out

    sends_halo = jnp.logical_and(g == GROUPS - 1, seg < last)

    @pl.when(sends_halo)
    def _():
        for copy in halo_copies():
            copy.start()

    params = [(cw_in, cw.at[:, lanes(f, cw_in.shape[1])]), (gn_in, gn.at[:, lanes(f, gn_in.shape[1])])]

    def small(p):
        return [(x.at[:, b_at(p)], raw_bc.at[mine, 0:N]),
                (x.at[:, c_at(p)], raw_bc.at[mine, N : 2 * N]), (dt, dts.at[g])]

    first = []
    for d in range(1, nf):
        for k, (src, dst) in enumerate(params):
            first.append(pltpu.make_async_remote_copy(
                src, dst, psend.at[d, k], precv.at[d, k], device_id=sibling(d)))
    for d in (2, 1, 3):
        for k, (src, dst) in enumerate(small(lax.rem(g + d, GROUPS))):
            first.append(pltpu.make_async_remote_copy(
                src, dst, bsend.at[d, k], brecv.at[d, k], device_id=peer(d)))
    for k, (src, dst) in enumerate(small(g) + params):
        first.append(pltpu.make_async_copy(src, dst, own_sem.at[k]))
    for copy in first:
        copy.start()

    def pieces(q):
        out = []
        for d in (2, 1, 3):
            p = lax.rem(g + d, GROUPS)
            out.append(pltpu.make_async_remote_copy(
                x.at[:, lanes(p * chunks + q, WIDTH)], raw.at[q, mine], xsend.at[d, q],
                xrecv.at[d, q], device_id=peer(d)))
        out.append(pltpu.make_async_copy(
            x.at[:, lanes(g * chunks + q, WIDTH)], raw.at[q, mine], xown.at[q]))
        return out

    @pl.loop(0, chunks)
    def _(q):
        for copy in pieces(q):
            copy.start()

    @pl.when(seg == 0)
    def _():
        q_buf[...] = jnp.zeros_like(q_buf)

    fill_selection(sel, g)
    squares[...] = jnp.zeros_like(squares)
    for copy in first:
        copy.wait()

    @pl.when(seg > 0)
    def _():
        for copy in halo_copies()[:3]:
            copy.wait_recv()

    def before(at, size):
        return jnp.where(seg > 0, halo[HALO - 8 :, at].astype(F32), 0.0)

    ext[0:8, :] = before(pl.ds(gw, 2 * N), 2 * N)
    ext[8:, :] = raw_bc[...].astype(F32)
    keys[...] = silu_conv(ext, 0, cw, b_at(g), N)
    queries = silu_conv(ext, N, cw, c_at(g), N)
    owner = lax.broadcasted_iota(jnp.int32, (3, heads), 1) // (heads // nf)
    vectors = cw[5:8, 0:heads]
    for d in range(1, nf):
        vectors = jnp.where(owner == d, cw[5:8, pl.ds(d * cw_in.shape[1], heads)], vectors)
    lower = (lax.broadcasted_iota(jnp.int32, (rows, rows), 0)
             >= lax.broadcasted_iota(jnp.int32, (rows, rows), 1))
    ones = jnp.where(lower, 1.0, 0.0)
    scale = jnp.exp(vectors[1:2, :])
    decayed = jnp.ones((1, heads), F32)
    for j in range(GROUPS):
        at = pl.ds(j * rows, rows)
        delta = dts[j].astype(F32) + vectors[0:1, :]
        delta = jnp.maximum(delta, 0.0) + jnp.log1p(jnp.exp(-jnp.abs(delta)))
        cum = lax.dot_general(ones, -scale * delta, (((1,), (0,)), ((), ())),
                              precision=lax.Precision.HIGHEST, preferred_element_type=F32)
        decay = jnp.exp(cum)
        source[j] = hi_lo(delta * jnp.exp(-cum))
        decay_2[j] = hi_lo(decay)
        carry_2[j] = hi_lo(decay * decayed)
        block_decay = decay[rows - 1 : rows, :]
        decayed = decayed * block_decay
        vec_2[j] = hi_lo(jnp.concatenate(
            [vectors[2:3, :], block_decay, decayed, jnp.zeros((5, heads), F32)], axis=0))
        mine_q = queries[j * rows : (j + 1) * rows]
        scores = jnp.where(lower, dot(mine_q, keys[at, :], ((1,), (1,))), 0.0).astype(BF16)
        left[j] = jnp.concatenate([scores, mine_q], axis=1)

    def local_step(q):
        for copy in pieces(q)[:3]:
            copy.wait_recv()
        pieces(q)[3].wait()
        here = lanes(q, WIDTH)
        ext[0:8, :] = before(here, WIDTH)
        ext[8:, :] = raw[q].astype(F32)
        act = silu_conv(ext, 0, cw, lanes(g * chunks + q, WIDTH), WIDTH)
        pick = sel[:, here]
        state = jnp.zeros((N, WIDTH), F32)
        for j in range(GROUPS):
            values = act[j * rows : (j + 1) * rows].astype(F32)
            weighted = (values * dot(source[j], pick)).astype(BF16)
            vec = dot(vec_2[j], pick)
            inner = dot(left[j], jnp.concatenate([weighted, state.astype(BF16)], axis=0))
            z_buf[q, j] = dot(decay_2[j], pick) * inner + vec[0:1, :] * values
            state = vec[1:2, :] * (state + dot(keys[pl.ds(j * rows, rows), :], weighted, ((0,), (0,))))
        p_buf[q] = state

    def hop(q):
        return pltpu.make_async_remote_copy(
            r_buf.at[q], q_buf.at[q], csend.at[q], crecv.at[q], device_id=device(seg + 1, g, nz))

    def back(d, q):
        return pltpu.make_async_remote_copy(
            y_out.at[lax.rem(g + d, GROUPS), q], y_in.at[g, q], osend.at[d, q], orecv.at[d, q],
            device_id=peer(d))

    def carry_step(q):
        pick = sel[:, lanes(q, WIDTH)]

        @pl.when(seg > 0)
        def _():
            hop(q).wait_recv()

        state = q_buf[q]

        @pl.when(seg < last)
        def _():
            through = dot(vec_2[GROUPS - 1], pick)[2:3, :]
            r_buf[q] = (p_buf[q] + through * state.astype(F32)).astype(r_buf.dtype)
            hop(q).start()

        low = state.astype(BF16)
        for j in range(GROUPS):
            carried = dot(left[j, :, N:], low) * dot(carry_2[j], pick)
            y_out[j, q] = (z_buf[q, j] + carried).astype(BF16)
        for d in range(1, GROUPS):
            back(d, q).start()
        y_in[g, q] = y_out[g, q]

    lag = seg if nz * nf <= chunks else jnp.where(seg < chunks, seg, chunks)

    @pl.loop(0, 2 * chunks)
    def _(i):
        @pl.when(i < chunks)
        def _():
            local_step(i)

        @pl.when(jnp.logical_and(i >= lag, i < lag + chunks))
        def _():
            carry_step(i - lag)

    @pl.loop(0, chunks)
    def _(q):
        for d in range(1, GROUPS):
            back(d, q).wait_recv()
        for p in range(GROUPS):
            y = y_in[p, q].astype(F32)
            squares[p] = squares[p] + y * y

    def finished(p):
        at = lanes(p, gw)
        return pltpu.make_async_copy(o_buf.at[:, at], out.at[:, at], out_sem.at[p])

    @pl.loop(0, GROUPS)
    def _(p):
        norm = lax.rsqrt(jnp.sum(squares[p], axis=1, keepdims=True) * (1.0 / gw) + 1e-05)
        for q in range(chunks):
            at = lanes(p * chunks + q, WIDTH)
            o_buf[:, at] = (y_in[p, q].astype(F32) * norm * gn[0:1, at]).astype(BF16)
        finished(p).start()

    @pl.loop(0, chunks)
    def _(q):
        for copy in pieces(q)[:3]:
            copy.wait_send()
        for d in range(1, GROUPS):
            back(d, q).wait_send()

    @pl.when(seg < last)
    def _():
        @pl.loop(0, chunks)
        def _(q):
            hop(q).wait_send()

    @pl.when(sends_halo)
    def _():
        for copy in halo_copies():
            copy.wait_send()

    for p in range(GROUPS):
        finished(p).wait()


def mixer(x, dt, cw, gn):
    rows, ch = x.shape
    heads = dt.shape[1]
    nf = lax.axis_size("fsdp")
    segments = nf * (lax.axis_size("ctx") // GROUPS)
    gw = heads * P_SIZE // GROUPS
    chunks = gw // WIDTH
    length = rows * GROUPS
    link = BF16 if segments <= 8 else F32
    vm, dma = pltpu.VMEM, pltpu.SemaphoreType.DMA
    return pl.pallas_call(
        mixer_kernel,
        out_shape=jax.ShapeDtypeStruct((rows, gw * GROUPS), BF16),
        in_specs=[ANY] * 4,
        out_specs=ANY,
        scratch_shapes=[
            vm((chunks, length, WIDTH), BF16),
            vm((length, 2 * N), BF16),
            vm((GROUPS, rows, heads), BF16),
            vm((HALO, gw + 2 * N), BF16),
            vm((8, ch), F32),
            vm((1, gw * GROUPS), F32),
            vm((2 * heads, gw), BF16),
            vm((8 + length, WIDTH), F32),
            vm((length, N), BF16),
            vm((GROUPS, rows, 2 * N), BF16),
            vm((GROUPS, rows, 2 * heads), BF16),
            vm((GROUPS, rows, 2 * heads), BF16),
            vm((GROUPS, rows, 2 * heads), BF16),
            vm((GROUPS, 8, 2 * heads), BF16),
            vm((chunks, GROUPS, rows, WIDTH), F32),
            vm((chunks, N, WIDTH), F32),
            vm((chunks, N, WIDTH), link),
            vm((chunks, N, WIDTH), link),
            vm((GROUPS, chunks, rows, WIDTH), BF16),
            vm((GROUPS, chunks, rows, WIDTH), BF16),
            vm((rows, gw * GROUPS), BF16),
            vm((GROUPS, rows, WIDTH), F32),
            dma((GROUPS, chunks)), dma((GROUPS, chunks)), dma((GROUPS, 3)), dma((GROUPS, 3)),
            dma((nf, 2)), dma((nf, 2)), dma((GROUPS, 3)), dma((3,)),
            dma((chunks,)), dma((chunks,)), dma((GROUPS, chunks)), dma((GROUPS, chunks)),
            dma((chunks,)), dma((5,)), dma((GROUPS,)),
        ],
        compiler_params=pltpu.CompilerParams(
            collective_id=0, has_side_effects=True, vmem_limit_bytes=62 << 20),
        name="mixer",
    )(x, dt, cw, gn)


def local(xbc, dt, conv_weight, conv_bias, dt_bias, a_log, skip, norm_gain):
    width, own = conv_bias.shape[0], dt_bias.shape[0]
    shape = (8, width)
    row = lax.broadcasted_iota(jnp.int32, shape, 0)
    params = lax.pad(conv_weight, 0.0, ((0, 4, 0), (0, 0, 0)))
    params = jnp.where(row == 4, jnp.broadcast_to(conv_bias, shape), params)
    for k, vector in enumerate((dt_bias, a_log, skip)):
        repeated = sum(lax.pad(vector, 0.0, ((at, width - own - at, 0),))
                       for at in range(0, dt.shape[1], own))
        params = jnp.where(row == 5 + k, jnp.broadcast_to(repeated, shape), params)
    return mixer(xbc, dt, params, norm_gain[None])


def solution(mesh):
    placed = (
        P(("fsdp", "ctx"), None),
        P(("fsdp", "ctx"), None),
        P(None, "fsdp"),
        P("fsdp"),
        P("fsdp"),
        P("fsdp"),
        P("fsdp"),
        P("fsdp"),
    )
    return jax.shard_map(
        local, mesh=mesh, in_specs=placed, out_specs=P(("fsdp", "ctx"), None), check_vma=False
    )
```

```python
import jax
import jax.numpy as jnp
from jax import lax
from jax.experimental import pallas as pl
from jax.experimental.pallas import tpu as pltpu
from jax.sharding import PartitionSpec as P

P_SIZE = 64
N = 128
GROUPS = 4
HALO = 16
WIDTH = 256
F32, BF16 = jnp.float32, jnp.bfloat16
ANY = pl.BlockSpec(memory_space=pl.ANY)


def place():
    f, c = lax.axis_index("fsdp"), lax.axis_index("ctx")
    nz = lax.axis_size("ctx") // GROUPS
    nf = lax.axis_size("fsdp")
    g, z = lax.rem(c, GROUPS), c // GROUPS
    return f, c, g, z, nz, nf, f * nz + z


def device(seg, g, nz):
    return {"fsdp": seg // nz, "ctx": lax.rem(seg, nz) * GROUPS + g}


def lanes(index, size):
    return pl.ds(pl.multiple_of(index * size, 128), size)


def hi_lo(v):
    hi = v.astype(BF16)
    return jnp.concatenate([hi, (v - hi.astype(F32)).astype(BF16)], axis=1)


def dot(a, b, dims=((1,), (0,))):
    return lax.dot_general(a, b, (dims, ((), ())), preferred_element_type=F32)


def fill_selection(sel, g):
    heads, width = sel.shape[0] // 2, sel.shape[1]
    per_group = width // P_SIZE
    row = lax.broadcasted_iota(jnp.int32, sel.shape, 0)
    col = lax.broadcasted_iota(jnp.int32, sel.shape, 1)
    row = jnp.where(row >= heads, row - heads, row)
    sel[...] = jnp.where(row == g * per_group + col // P_SIZE, 1.0, 0.0).astype(BF16)


def silu_conv(ext, start, cw, at, size):
    rows = ext.shape[0] - 8
    total = cw[4:5, at]
    for k in range(4):
        total = total + cw[k : k + 1, at] * ext[5 + k : 5 + k + rows, start : start + size]
    return (total / (1.0 + jnp.exp(-total))).astype(BF16)


def mixer_kernel(x, dt, cw_in, gn_in, out,
                 raw, raw_bc, dts, halo, cw, gn, sel, ext, keys, left, source, decay_2, carry_2,
                 vec_2, z_buf, p_buf, q_buf, r_buf, y_out, y_in, o_buf, squares,
                 xsend, xrecv, bsend, brecv, psend, precv, hsend, hrecv, csend, crecv,
                 osend, orecv, xown, own_sem, out_sem):
    f, c, g, z, nz, nf, seg = place()
    last = nz * nf - 1
    rows = x.shape[0]
    chunks = raw.shape[0]
    gw = chunks * WIDTH
    di = gw * GROUPS
    heads = dt.shape[1]

    def peer(d):
        return {"fsdp": f, "ctx": z * GROUPS + lax.rem(g + d, GROUPS)}

    def sibling(d):
        return {"fsdp": lax.rem(f + d, nf), "ctx": c}

    barrier = pltpu.get_barrier_semaphore()
    for d in range(1, GROUPS):
        pl.semaphore_signal(barrier, inc=1, device_id=peer(d))
    for d in range(1, nf):
        pl.semaphore_signal(barrier, inc=1, device_id=sibling(d))

    @pl.when(seg > 0)
    def _():
        pl.semaphore_signal(barrier, inc=1, device_id=device(seg - 1, g, nz))

    @pl.when(jnp.logical_and(seg > 0, g < GROUPS - 1))
    def _():
        pl.semaphore_signal(barrier, inc=1, device_id=device(seg - 1, GROUPS - 1, nz))

    more = jnp.where(seg < last, jnp.where(g == GROUPS - 1, GROUPS, 1), 0)
    pl.semaphore_wait(barrier, GROUPS - 1 + nf - 1 + more)

    def b_at(p):
        return pl.ds(pl.multiple_of(di + p * N, 128), N)

    def c_at(p):
        return pl.ds(pl.multiple_of(di + (GROUPS + p) * N, 128), N)

    mine = pl.ds(pl.multiple_of(g * rows, 128), rows)

    def halo_copies():
        out = []
        tail = pl.ds(rows - HALO, HALO)
        for p in range(GROUPS):
            parts = [(x.at[tail, lanes(p, gw)], halo.at[:, 0:gw]),
                     (x.at[tail, b_at(p)], halo.at[:, gw : gw + N]),
                     (x.at[tail, c_at(p)], halo.at[:, gw + N : gw + 2 * N])]
            for k, (src, dst) in enumerate(parts):
                out.append(pltpu.make_async_remote_copy(
                    src, dst, hsend.at[p, k], hrecv.at[k], device_id=device(seg + 1, p, nz)))
        return out

    sends_halo = jnp.logical_and(g == GROUPS - 1, seg < last)

    @pl.when(sends_halo)
    def _():
        for copy in halo_copies():
            copy.start()

    params = [(cw_in, cw.at[:, lanes(f, cw_in.shape[1])]), (gn_in, gn.at[:, lanes(f, gn_in.shape[1])])]

    def small(p):
        return [(x.at[:, b_at(p)], raw_bc.at[mine, 0:N]),
                (x.at[:, c_at(p)], raw_bc.at[mine, N : 2 * N]), (dt, dts.at[g])]

    first = []
    for d in range(1, nf):
        for k, (src, dst) in enumerate(params):
            first.append(pltpu.make_async_remote_copy(
                src, dst, psend.at[d, k], precv.at[d, k], device_id=sibling(d)))
    for d in (2, 1, 3):
        for k, (src, dst) in enumerate(small(lax.rem(g + d, GROUPS))):
            first.append(pltpu.make_async_remote_copy(
                src, dst, bsend.at[d, k], brecv.at[d, k], device_id=peer(d)))
    for k, (src, dst) in enumerate(small(g) + params):
        first.append(pltpu.make_async_copy(src, dst, own_sem.at[k]))
    for copy in first:
        copy.start()

    def pieces(q):
        out = []
        for d in (2, 1, 3):
            p = lax.rem(g + d, GROUPS)
            out.append(pltpu.make_async_remote_copy(
                x.at[:, lanes(p * chunks + q, WIDTH)], raw.at[q, mine], xsend.at[d, q],
                xrecv.at[d, q], device_id=peer(d)))
        out.append(pltpu.make_async_copy(
            x.at[:, lanes(g * chunks + q, WIDTH)], raw.at[q, mine], xown.at[q]))
        return out

    @pl.loop(0, chunks)
    def _(q):
        for copy in pieces(q):
            copy.start()

    @pl.when(seg == 0)
    def _():
        q_buf[...] = jnp.zeros_like(q_buf)

    fill_selection(sel, g)
    squares[...] = jnp.zeros_like(squares)
    for copy in first:
        copy.wait()

    @pl.when(seg > 0)
    def _():
        for copy in halo_copies()[:3]:
            copy.wait_recv()

    def before(at, size):
        return jnp.where(seg > 0, halo[HALO - 8 :, at].astype(F32), 0.0)

    ext[0:8, :] = before(pl.ds(gw, 2 * N), 2 * N)
    ext[8:, :] = raw_bc[...].astype(F32)
    keys[...] = silu_conv(ext, 0, cw, b_at(g), N)
    queries = silu_conv(ext, N, cw, c_at(g), N)
    vectors = cw[5:8, 0:heads]
    for d in range(1, nf):
        vectors = vectors + cw[5:8, pl.ds(d * cw_in.shape[1], heads)]
    lower = (lax.broadcasted_iota(jnp.int32, (rows, rows), 0)
             >= lax.broadcasted_iota(jnp.int32, (rows, rows), 1))
    ones = jnp.where(lower, 1.0, 0.0)
    scale = jnp.exp(vectors[1:2, :])
    decayed = jnp.ones((1, heads), F32)
    for j in range(GROUPS):
        at = pl.ds(j * rows, rows)
        delta = dts[j].astype(F32) + vectors[0:1, :]
        delta = jnp.maximum(delta, 0.0) + jnp.log1p(jnp.exp(-jnp.abs(delta)))
        cum = lax.dot_general(ones, -scale * delta, (((1,), (0,)), ((), ())),
                              precision=lax.Precision.HIGHEST, preferred_element_type=F32)
        decay = jnp.exp(cum)
        source[j] = hi_lo(delta * jnp.exp(-cum))
        decay_2[j] = hi_lo(decay)
        carry_2[j] = hi_lo(decay * decayed)
        block_decay = decay[rows - 1 : rows, :]
        decayed = decayed * block_decay
        vec_2[j] = hi_lo(jnp.concatenate(
            [vectors[2:3, :], block_decay, decayed, jnp.zeros((5, heads), F32)], axis=0))
        mine_q = queries[j * rows : (j + 1) * rows]
        scores = jnp.where(lower, dot(mine_q, keys[at, :], ((1,), (1,))), 0.0).astype(BF16)
        left[j] = jnp.concatenate([scores, mine_q], axis=1)

    def local_step(q):
        for copy in pieces(q)[:3]:
            copy.wait_recv()
        pieces(q)[3].wait()
        here = lanes(q, WIDTH)
        ext[0:8, :] = before(here, WIDTH)
        ext[8:, :] = raw[q].astype(F32)
        act = silu_conv(ext, 0, cw, lanes(g * chunks + q, WIDTH), WIDTH)
        pick = sel[:, here]
        state = jnp.zeros((N, WIDTH), F32)
        for j in range(GROUPS):
            values = act[j * rows : (j + 1) * rows].astype(F32)
            weighted = (values * dot(source[j], pick)).astype(BF16)
            vec = dot(vec_2[j], pick)
            inner = dot(left[j], jnp.concatenate([weighted, state.astype(BF16)], axis=0))
            z_buf[q, j] = dot(decay_2[j], pick) * inner + vec[0:1, :] * values
            state = vec[1:2, :] * (state + dot(keys[pl.ds(j * rows, rows), :], weighted, ((0,), (0,))))
        p_buf[q] = state

    def hop(q):
        return pltpu.make_async_remote_copy(
            r_buf.at[q], q_buf.at[q], csend.at[q], crecv.at[q], device_id=device(seg + 1, g, nz))

    def back(d, q):
        return pltpu.make_async_remote_copy(
            y_out.at[lax.rem(g + d, GROUPS), q], y_in.at[g, q], osend.at[d, q], orecv.at[d, q],
            device_id=peer(d))

    def carry_step(q):
        pick = sel[:, lanes(q, WIDTH)]

        @pl.when(seg > 0)
        def _():
            hop(q).wait_recv()

        state = q_buf[q]

        @pl.when(seg < last)
        def _():
            through = dot(vec_2[GROUPS - 1], pick)[2:3, :]
            r_buf[q] = (p_buf[q] + through * state.astype(F32)).astype(r_buf.dtype)
            hop(q).start()

        low = state.astype(BF16)
        for j in range(GROUPS):
            carried = dot(left[j, :, N:], low) * dot(carry_2[j], pick)
            y_out[j, q] = (z_buf[q, j] + carried).astype(BF16)
        for d in range(1, GROUPS):
            back(d, q).start()
        y_in[g, q] = y_out[g, q]

    lag = seg if nz * nf <= chunks else jnp.where(seg < chunks, seg, chunks)

    @pl.loop(0, 2 * chunks)
    def _(i):
        @pl.when(i < chunks)
        def _():
            local_step(i)

        @pl.when(jnp.logical_and(i >= lag, i < lag + chunks))
        def _():
            carry_step(i - lag)

    @pl.loop(0, chunks)
    def _(q):
        for d in range(1, GROUPS):
            back(d, q).wait_recv()
        for p in range(GROUPS):
            y = y_in[p, q].astype(F32)
            squares[p] = squares[p] + y * y

    def finished(p):
        at = lanes(p, gw)
        return pltpu.make_async_copy(o_buf.at[:, at], out.at[:, at], out_sem.at[p])

    @pl.loop(0, GROUPS)
    def _(p):
        norm = lax.rsqrt(jnp.sum(squares[p], axis=1, keepdims=True) * (1.0 / gw) + 1e-05)
        for q in range(chunks):
            at = lanes(p * chunks + q, WIDTH)
            o_buf[:, at] = (y_in[p, q].astype(F32) * norm * gn[0:1, at]).astype(BF16)
        finished(p).start()

    @pl.loop(0, chunks)
    def _(q):
        for copy in pieces(q)[:3]:
            copy.wait_send()
        for d in range(1, GROUPS):
            back(d, q).wait_send()

    @pl.when(seg < last)
    def _():
        @pl.loop(0, chunks)
        def _(q):
            hop(q).wait_send()

    @pl.when(sends_halo)
    def _():
        for copy in halo_copies():
            copy.wait_send()

    for p in range(GROUPS):
        finished(p).wait()


def mixer(x, dt, cw, gn):
    rows, ch = x.shape
    heads = dt.shape[1]
    nf = lax.axis_size("fsdp")
    segments = nf * (lax.axis_size("ctx") // GROUPS)
    gw = heads * P_SIZE // GROUPS
    chunks = gw // WIDTH
    length = rows * GROUPS
    link = BF16 if segments <= 8 else F32
    vm, dma = pltpu.VMEM, pltpu.SemaphoreType.DMA
    return pl.pallas_call(
        mixer_kernel,
        out_shape=jax.ShapeDtypeStruct((rows, gw * GROUPS), BF16),
        in_specs=[ANY] * 4,
        out_specs=ANY,
        scratch_shapes=[
            vm((chunks, length, WIDTH), BF16),
            vm((length, 2 * N), BF16),
            vm((GROUPS, rows, heads), BF16),
            vm((HALO, gw + 2 * N), BF16),
            vm((8, ch), F32),
            vm((1, gw * GROUPS), F32),
            vm((2 * heads, gw), BF16),
            vm((8 + length, WIDTH), F32),
            vm((length, N), BF16),
            vm((GROUPS, rows, 2 * N), BF16),
            vm((GROUPS, rows, 2 * heads), BF16),
            vm((GROUPS, rows, 2 * heads), BF16),
            vm((GROUPS, rows, 2 * heads), BF16),
            vm((GROUPS, 8, 2 * heads), BF16),
            vm((chunks, GROUPS, rows, WIDTH), F32),
            vm((chunks, N, WIDTH), F32),
            vm((chunks, N, WIDTH), link),
            vm((chunks, N, WIDTH), link),
            vm((GROUPS, chunks, rows, WIDTH), BF16),
            vm((GROUPS, chunks, rows, WIDTH), BF16),
            vm((rows, gw * GROUPS), BF16),
            vm((GROUPS, rows, WIDTH), F32),
            dma((GROUPS, chunks)), dma((GROUPS, chunks)), dma((GROUPS, 3)), dma((GROUPS, 3)),
            dma((nf, 2)), dma((nf, 2)), dma((GROUPS, 3)), dma((3,)),
            dma((chunks,)), dma((chunks,)), dma((GROUPS, chunks)), dma((GROUPS, chunks)),
            dma((chunks,)), dma((5,)), dma((GROUPS,)),
        ],
        compiler_params=pltpu.CompilerParams(
            collective_id=0, has_side_effects=True, vmem_limit_bytes=51 << 20),
        name="mixer",
    )(x, dt, cw, gn)


def local(xbc, dt, conv_weight, conv_bias, dt_bias, a_log, skip, norm_gain):
    heads = dt.shape[1]
    own = dt_bias.shape[0]
    width = conv_bias.shape[0]
    small = lax.dynamic_update_slice(
        jnp.zeros((3, width), F32), jnp.stack([dt_bias, a_log, skip]),
        (0, lax.axis_index("fsdp") * own))
    params = jnp.concatenate([conv_weight, conv_bias[None], small], axis=0)
    return mixer(xbc, dt, params, norm_gain[None])


def solution(mesh):
    placed = (
        P(("fsdp", "ctx"), None),
        P(("fsdp", "ctx"), None),
        P(None, "fsdp"),
        P("fsdp"),
        P("fsdp"),
        P("fsdp"),
        P("fsdp"),
        P("fsdp"),
    )
    return jax.shard_map(
        local, mesh=mesh, in_specs=placed, out_specs=P(("fsdp", "ctx"), None), check_vma=False
    )
```

```python
import jax
import jax.numpy as jnp
from jax import lax
from jax.experimental import pallas as pl
from jax.experimental.pallas import tpu as pltpu
from jax.sharding import PartitionSpec as P

P_SIZE = 64
N = 128
GROUPS = 4
HALO = 16
WIDTH = 256
F32, BF16 = jnp.float32, jnp.bfloat16
ANY = pl.BlockSpec(memory_space=pl.ANY)


def place():
    f, c = lax.axis_index("fsdp"), lax.axis_index("ctx")
    nz = lax.axis_size("ctx") // GROUPS
    nf = lax.axis_size("fsdp")
    g, z = lax.rem(c, GROUPS), c // GROUPS
    return f, c, g, z, nz, nf, f * nz + z


def device(seg, g, nz):
    return {"fsdp": seg // nz, "ctx": lax.rem(seg, nz) * GROUPS + g}


def lanes(index, size):
    return pl.ds(pl.multiple_of(index * size, 128), size)


def hi_lo(v):
    hi = v.astype(BF16)
    return jnp.concatenate([hi, (v - hi.astype(F32)).astype(BF16)], axis=1)


def dot(a, b, dims=((1,), (0,))):
    return lax.dot_general(a, b, (dims, ((), ())), preferred_element_type=F32)


def fill_selection(sel, g):
    heads, width = sel.shape[0] // 2, sel.shape[1]
    per_group = width // P_SIZE
    row = lax.broadcasted_iota(jnp.int32, sel.shape, 0)
    col = lax.broadcasted_iota(jnp.int32, sel.shape, 1)
    row = jnp.where(row >= heads, row - heads, row)
    sel[...] = jnp.where(row == g * per_group + col // P_SIZE, 1.0, 0.0).astype(BF16)


def silu_conv(ext, start, cw, at, size):
    rows = ext.shape[0] - 8
    total = cw[4:5, at]
    for k in range(4):
        total = total + cw[k : k + 1, at] * ext[5 + k : 5 + k + rows, start : start + size]
    return (total / (1.0 + jnp.exp(-total))).astype(BF16)


def mixer_kernel(x, dt, cw_in, out,
                 raw, raw_bc, dts, halo, cw, sel, ext, keys, left, source, decay_2, carry_2,
                 vec_2, z_buf, p_buf, q_buf, r_buf, y_out, y_in, o_buf, squares,
                 xsend, xrecv, bsend, brecv, psend, precv, hsend, hrecv, csend, crecv,
                 osend, orecv, xown, own_sem, out_sem):
    f, c, g, z, nz, nf, seg = place()
    last = nz * nf - 1
    rows = x.shape[0]
    chunks = raw.shape[0]
    gw = chunks * WIDTH
    di = gw * GROUPS
    heads = dt.shape[1]

    def peer(d):
        return {"fsdp": f, "ctx": z * GROUPS + lax.rem(g + d, GROUPS)}

    def sibling(d):
        return {"fsdp": lax.rem(f + d, nf), "ctx": c}

    barrier = pltpu.get_barrier_semaphore()
    for d in range(1, GROUPS):
        pl.semaphore_signal(barrier, inc=1, device_id=peer(d))
    for d in range(1, nf):
        pl.semaphore_signal(barrier, inc=1, device_id=sibling(d))

    @pl.when(seg > 0)
    def _():
        pl.semaphore_signal(barrier, inc=1, device_id=device(seg - 1, g, nz))

    @pl.when(jnp.logical_and(seg > 0, g < GROUPS - 1))
    def _():
        pl.semaphore_signal(barrier, inc=1, device_id=device(seg - 1, GROUPS - 1, nz))

    more = jnp.where(seg < last, jnp.where(g == GROUPS - 1, GROUPS, 1), 0)
    pl.semaphore_wait(barrier, GROUPS - 1 + nf - 1 + more)

    def b_at(p):
        return pl.ds(pl.multiple_of(di + p * N, 128), N)

    def c_at(p):
        return pl.ds(pl.multiple_of(di + (GROUPS + p) * N, 128), N)

    mine = pl.ds(pl.multiple_of(g * rows, 128), rows)

    def halo_copies():
        out = []
        tail = pl.ds(rows - HALO, HALO)
        for p in range(GROUPS):
            parts = [(x.at[tail, lanes(p, gw)], halo.at[:, 0:gw]),
                     (x.at[tail, b_at(p)], halo.at[:, gw : gw + N]),
                     (x.at[tail, c_at(p)], halo.at[:, gw + N : gw + 2 * N])]
            for k, (src, dst) in enumerate(parts):
                out.append(pltpu.make_async_remote_copy(
                    src, dst, hsend.at[p, k], hrecv.at[k], device_id=device(seg + 1, p, nz)))
        return out

    sends_halo = jnp.logical_and(g == GROUPS - 1, seg < last)

    @pl.when(sends_halo)
    def _():
        for copy in halo_copies():
            copy.start()

    params = [(cw_in, cw.at[:, lanes(f, cw_in.shape[1])])]

    def small(p):
        return [(x.at[:, b_at(p)], raw_bc.at[mine, 0:N]),
                (x.at[:, c_at(p)], raw_bc.at[mine, N : 2 * N]), (dt, dts.at[g])]

    first = []
    for d in range(1, nf):
        for k, (src, dst) in enumerate(params):
            first.append(pltpu.make_async_remote_copy(
                src, dst, psend.at[d, k], precv.at[d, k], device_id=sibling(d)))
    for d in (2, 1, 3):
        for k, (src, dst) in enumerate(small(lax.rem(g + d, GROUPS))):
            first.append(pltpu.make_async_remote_copy(
                src, dst, bsend.at[d, k], brecv.at[d, k], device_id=peer(d)))
    for k, (src, dst) in enumerate(small(g) + params):
        first.append(pltpu.make_async_copy(src, dst, own_sem.at[k]))
    for copy in first:
        copy.start()

    def pieces(q):
        out = []
        for d in (2, 1, 3):
            p = lax.rem(g + d, GROUPS)
            out.append(pltpu.make_async_remote_copy(
                x.at[:, lanes(p * chunks + q, WIDTH)], raw.at[q, mine], xsend.at[d, q],
                xrecv.at[d, q], device_id=peer(d)))
        out.append(pltpu.make_async_copy(
            x.at[:, lanes(g * chunks + q, WIDTH)], raw.at[q, mine], xown.at[q]))
        return out

    @pl.loop(0, chunks)
    def _(q):
        for copy in pieces(q):
            copy.start()

    @pl.when(seg == 0)
    def _():
        q_buf[...] = jnp.zeros_like(q_buf)

    fill_selection(sel, g)
    squares[...] = jnp.zeros_like(squares)
    for copy in first:
        copy.wait()

    @pl.when(seg > 0)
    def _():
        for copy in halo_copies()[:3]:
            copy.wait_recv()

    def before(at, size):
        return jnp.where(seg > 0, halo[HALO - 8 :, at].astype(F32), 0.0)

    ext[0:8, :] = before(pl.ds(gw, 2 * N), 2 * N)
    ext[8:, :] = raw_bc[...].astype(F32)
    keys[...] = silu_conv(ext, 0, cw, b_at(g), N)
    queries = silu_conv(ext, N, cw, c_at(g), N)
    vectors = cw[5:6, 0 : 3 * heads]
    for d in range(1, nf):
        vectors = vectors + cw[5:6, pl.ds(d * cw_in.shape[1], 3 * heads)]
    step_bias, rate_log, direct = (vectors[:, k * heads : (k + 1) * heads] for k in range(3))
    lower = (lax.broadcasted_iota(jnp.int32, (rows, rows), 0)
             >= lax.broadcasted_iota(jnp.int32, (rows, rows), 1))
    ones = jnp.where(lower, 1.0, 0.0)
    scale = jnp.exp(rate_log)
    decayed = jnp.ones((1, heads), F32)
    for j in range(GROUPS):
        at = pl.ds(j * rows, rows)
        delta = dts[j].astype(F32) + step_bias
        delta = jnp.maximum(delta, 0.0) + jnp.log1p(jnp.exp(-jnp.abs(delta)))
        cum = lax.dot_general(ones, -scale * delta, (((1,), (0,)), ((), ())),
                              precision=lax.Precision.HIGHEST, preferred_element_type=F32)
        decay = jnp.exp(cum)
        source[j] = hi_lo(delta * jnp.exp(-cum))
        decay_2[j] = hi_lo(decay)
        carry_2[j] = hi_lo(decay * decayed)
        block_decay = decay[rows - 1 : rows, :]
        decayed = decayed * block_decay
        vec_2[j] = hi_lo(jnp.concatenate(
            [direct, block_decay, decayed, jnp.zeros((5, heads), F32)], axis=0))
        mine_q = queries[j * rows : (j + 1) * rows]
        scores = jnp.where(lower, dot(mine_q, keys[at, :], ((1,), (1,))), 0.0).astype(BF16)
        left[j] = jnp.concatenate([scores, mine_q], axis=1)

    def local_step(q):
        for copy in pieces(q)[:3]:
            copy.wait_recv()
        pieces(q)[3].wait()
        here = lanes(q, WIDTH)
        ext[0:8, :] = before(here, WIDTH)
        ext[8:, :] = raw[q].astype(F32)
        act = silu_conv(ext, 0, cw, lanes(g * chunks + q, WIDTH), WIDTH)
        pick = sel[:, here]
        state = jnp.zeros((N, WIDTH), F32)
        for j in range(GROUPS):
            values = act[j * rows : (j + 1) * rows].astype(F32)
            weighted = (values * dot(source[j], pick)).astype(BF16)
            vec = dot(vec_2[j], pick)
            inner = dot(left[j], jnp.concatenate([weighted, state.astype(BF16)], axis=0))
            z_buf[q, j] = dot(decay_2[j], pick) * inner + vec[0:1, :] * values
            state = vec[1:2, :] * (state + dot(keys[pl.ds(j * rows, rows), :], weighted, ((0,), (0,))))
        p_buf[q] = state

    def hop(q):
        return pltpu.make_async_remote_copy(
            r_buf.at[q], q_buf.at[q], csend.at[q], crecv.at[q], device_id=device(seg + 1, g, nz))

    def back(d, q):
        return pltpu.make_async_remote_copy(
            y_out.at[lax.rem(g + d, GROUPS), q], y_in.at[g, q], osend.at[d, q], orecv.at[d, q],
            device_id=peer(d))

    def carry_step(q):
        pick = sel[:, lanes(q, WIDTH)]

        @pl.when(seg > 0)
        def _():
            hop(q).wait_recv()

        state = q_buf[q]

        @pl.when(seg < last)
        def _():
            through = dot(vec_2[GROUPS - 1], pick)[2:3, :]
            r_buf[q] = (p_buf[q] + through * state.astype(F32)).astype(r_buf.dtype)
            hop(q).start()

        low = state.astype(BF16)
        for j in range(GROUPS):
            carried = dot(left[j, :, N:], low) * dot(carry_2[j], pick)
            y_out[j, q] = (z_buf[q, j] + carried).astype(BF16)
        for d in range(1, GROUPS):
            back(d, q).start()
        y_in[g, q] = y_out[g, q]

    lag = seg if nz * nf <= chunks else jnp.where(seg < chunks, seg, chunks)

    @pl.loop(0, 2 * chunks)
    def _(i):
        @pl.when(i < chunks)
        def _():
            local_step(i)

        @pl.when(jnp.logical_and(i >= lag, i < lag + chunks))
        def _():
            carry_step(i - lag)

    @pl.loop(0, chunks)
    def _(q):
        for d in range(1, GROUPS):
            back(d, q).wait_recv()
        for p in range(GROUPS):
            y = y_in[p, q].astype(F32)
            squares[p] = squares[p] + y * y

    def finished(p):
        at = lanes(p, gw)
        return pltpu.make_async_copy(o_buf.at[:, at], out.at[:, at], out_sem.at[p])

    per = di // nf // WIDTH

    def gain_of(i):
        at = i // per * cw_in.shape[1] + lax.rem(i, per) * WIDTH
        return cw[6:7, pl.ds(pl.multiple_of(at, 128), WIDTH)]

    @pl.loop(0, GROUPS)
    def _(p):
        norm = lax.rsqrt(jnp.sum(squares[p], axis=1, keepdims=True) * (1.0 / gw) + 1e-05)
        for q in range(chunks):
            at = lanes(p * chunks + q, WIDTH)
            o_buf[:, at] = (y_in[p, q].astype(F32) * norm * gain_of(p * chunks + q)).astype(BF16)
        finished(p).start()

    @pl.loop(0, chunks)
    def _(q):
        for copy in pieces(q)[:3]:
            copy.wait_send()
        for d in range(1, GROUPS):
            back(d, q).wait_send()

    @pl.when(seg < last)
    def _():
        @pl.loop(0, chunks)
        def _(q):
            hop(q).wait_send()

    @pl.when(sends_halo)
    def _():
        for copy in halo_copies():
            copy.wait_send()

    for p in range(GROUPS):
        finished(p).wait()


def mixer(x, dt, cw):
    rows, ch = x.shape
    heads = dt.shape[1]
    nf = lax.axis_size("fsdp")
    segments = nf * (lax.axis_size("ctx") // GROUPS)
    gw = heads * P_SIZE // GROUPS
    chunks = gw // WIDTH
    length = rows * GROUPS
    link = BF16 if segments <= 8 else F32
    vm, dma = pltpu.VMEM, pltpu.SemaphoreType.DMA
    return pl.pallas_call(
        mixer_kernel,
        out_shape=jax.ShapeDtypeStruct((rows, gw * GROUPS), BF16),
        in_specs=[ANY] * 3,
        out_specs=ANY,
        scratch_shapes=[
            vm((chunks, length, WIDTH), BF16),
            vm((length, 2 * N), BF16),
            vm((GROUPS, rows, heads), BF16),
            vm((HALO, gw + 2 * N), BF16),
            vm((8, ch), F32),
            vm((2 * heads, gw), BF16),
            vm((8 + length, WIDTH), F32),
            vm((length, N), BF16),
            vm((GROUPS, rows, 2 * N), BF16),
            vm((GROUPS, rows, 2 * heads), BF16),
            vm((GROUPS, rows, 2 * heads), BF16),
            vm((GROUPS, rows, 2 * heads), BF16),
            vm((GROUPS, 8, 2 * heads), BF16),
            vm((chunks, GROUPS, rows, WIDTH), F32),
            vm((chunks, N, WIDTH), F32),
            vm((chunks, N, WIDTH), link),
            vm((chunks, N, WIDTH), link),
            vm((GROUPS, chunks, rows, WIDTH), BF16),
            vm((GROUPS, chunks, rows, WIDTH), BF16),
            vm((rows, gw * GROUPS), BF16),
            vm((GROUPS, rows, WIDTH), F32),
            dma((GROUPS, chunks)), dma((GROUPS, chunks)), dma((GROUPS, 3)), dma((GROUPS, 3)),
            dma((nf, 1)), dma((nf, 1)), dma((GROUPS, 3)), dma((3,)),
            dma((chunks,)), dma((chunks,)), dma((GROUPS, chunks)), dma((GROUPS, chunks)),
            dma((chunks,)), dma((4,)), dma((GROUPS,)),
        ],
        compiler_params=pltpu.CompilerParams(
            collective_id=0, has_side_effects=True, vmem_limit_bytes=51 << 20),
        name="mixer",
    )(x, dt, cw)


def local(xbc, dt, conv_weight, conv_bias, dt_bias, a_log, skip, norm_gain):
    heads = dt.shape[1]
    own = dt_bias.shape[0]
    width = conv_bias.shape[0]
    small = lax.dynamic_update_slice(
        jnp.zeros((3, heads), F32), jnp.stack([dt_bias, a_log, skip]),
        (0, lax.axis_index("fsdp") * own)).reshape(1, 3 * heads)
    params = jnp.concatenate([
        conv_weight, conv_bias[None],
        jnp.pad(small, ((0, 0), (0, width - 3 * heads))),
        jnp.pad(norm_gain[None], ((0, 1), (0, width - norm_gain.shape[0]))),
    ], axis=0)
    return mixer(xbc, dt, params)


def solution(mesh):
    placed = (
        P(("fsdp", "ctx"), None),
        P(("fsdp", "ctx"), None),
        P(None, "fsdp"),
        P("fsdp"),
        P("fsdp"),
        P("fsdp"),
        P("fsdp"),
        P("fsdp"),
    )
    return jax.shard_map(
        local, mesh=mesh, in_specs=placed, out_specs=P(("fsdp", "ctx"), None), check_vma=False
    )
```
